32 devices in a mesh: fz: 8 (over y, x, core), fxy: 4 (over z).
Axes of the slice: x: 2, y: 2, z: 4, core: 2. Of those that a mesh axis runs over, the one named last changes fastest.
Arguments:
- e_field: float32 [3, 64, 64, 512], P(None, 'fz', 'fxy'), may hold values from -6 to 6
- h_field: float32 [3, 64, 64, 512], P(None, 'fz', 'fxy'), may hold values from -6 to 6
- e_decay: float32 [64, 64, 512], P('fz', 'fxy'), may hold values from 0.6 to 1
- e_gain: float32 [64, 64, 512], P('fz', 'fxy'), may hold values from 0.2 to 0.6
- port_cell: int32 [8, 256], P('fz', 'fxy'), may hold values from 0 to 65535
- port_node: int32 [8, 256], P('fz', 'fxy'), may hold values from 0 to 2047
- port_conductance: float32 [8, 256], P('fz', 'fxy'), may hold values from 0.5 to 2
- inverse: float32 [8, 2048, 2048], P('fz', 'fxy'), may hold values from -1 to 2, as said below
- line_near: int32 [8, 128], P('fz'), may hold values from 0 to 2047
- line_far: int32 [8, 128], P('fz'), may hold values from 0 to 2047
- line_delay: int32 [8, 128], P('fz'), may hold values from 1 to 6
- line_imped: float32 [8, 128], P('fz'), may hold values from 0.5 to 4
- hist_near: float32 [8, 6, 128], P('fz'), may hold values from -6 to 6
- hist_far: float32 [8, 6, 128], P('fz'), may hold values from -6 to 6
Outputs:
- e_out: float32 [3, 64, 64, 512], P(None, 'fz', 'fxy')
- h_out: float32 [3, 64, 64, 512], P(None, 'fz', 'fxy')
- node_volt: float32 [8, 2048], P('fz', 'fxy')
- line_wave: float32 [8, 2, 128], P('fz')
The draws below stay inside these ranges and needn't reach their ends.
Inputs may be any that keep to these rules, and one draw needn't show every extreme that they name: inverse[s] is symmetric for every s.
All inputs are finite; a program needn't handle non-finite values.
Results may differ from the reference program's by a relative error of at most 0.00029.
Values sent between devices are 32-bit elements; how exact they have to be, the bound alone decides.
A program may use at most 64 MiB of HBM per device.

```python
import math
import jax
import jax.numpy as jnp
from jax import lax

CZ = 8
CX = 16
NY = 512
NODES = 2048
PORTS_DEV = 64
LINES = 128
DMAX = 6
STEPS = 4
NZ = 64
NX = 64
PORTS = 256
N_FZ = 8


def draw_inverse(key, part):
    first, second = jax.random.split(jax.random.fold_in(key, 7))
    noise = jax.random.normal(first, (N_FZ, NODES, NODES), jnp.float32)
    symmetric = (noise + jnp.swapaxes(noise, 1, 2)) * (0.3 / math.sqrt(2.0 * NODES))
    diagonal = jax.random.uniform(second, (N_FZ, NODES), jnp.float32, 0.8, 1.2)
    return symmetric + diagonal[:, :, None] * jnp.eye(NODES, dtype=jnp.float32)


def with_ends(drawn, own_key, low, high):
    extent = drawn.shape
    place = [jax.random.randint(jax.random.fold_in(own_key, axis), (), 0, extent[axis]) for axis in range(len(extent))]
    drawn = drawn.at[tuple(place)].set(low)
    longest = extent.index(max(extent))
    place[longest] = (place[longest] + 1) % extent[longest]
    return drawn.at[tuple(place)].set(high)


def steps_of(key, shape, pieces, least, high):
    gain, own = 1.0, jax.random.fold_in(key, 6)
    for dim, parts in pieces:
        heights = jnp.exp(jax.random.uniform(jax.random.fold_in(own, dim), (parts,), jnp.float32, least / len(pieces), high / len(pieces)))
        gain = gain * jnp.repeat(heights, shape[dim] // parts).reshape([-1 if axis == dim else 1 for axis in range(len(shape))])
    return gain


def scatter_about(rng, dims, deviation, limit, cuts=(), held_as=jnp.bfloat16):
    array = jax.random.normal(rng, dims, jnp.float32) * deviation
    if len(cuts) > 0:
        array = steps_of(rng, dims, cuts, -0.22, 0.18) * array
    return jnp.clip(array, min=-limit, max=limit).astype(held_as)


def setup_inputs(seed: int = 0) -> dict:
    splits = jax.random.split(jax.random.key(seed), 15)
    e_field = scatter_about(splits[0], (3, NZ, NX, NY), 1.0, 6.0, ((1, 8), (2, 4)), jnp.float32)
    h_field = scatter_about(splits[1], (3, NZ, NX, NY), 1.0, 6.0, ((1, 8), (2, 4)), jnp.float32)
    e_decay = jnp.clip(0.6 + 0.39999998 * jax.random.uniform(splits[2], (NZ, NX, NY), jnp.float32) ** steps_of(splits[2], (NZ, NX, NY), ((0, 8), (1, 4)), -0.2, 0.2), 0.6, 1.0)
    e_gain = jnp.clip(0.2 + 0.400000021 * jax.random.uniform(splits[3], (NZ, NX, NY), jnp.float32) ** steps_of(splits[3], (NZ, NX, NY), ((0, 8), (1, 4)), -0.2, 0.2), 0.2, 0.6)
    port_cell = with_ends(jax.random.randint(splits[4], (N_FZ, PORTS), 0, CZ * CX * NY), jax.random.fold_in(splits[4], 1), 0, (CZ * CX * NY) - 1).astype(jnp.int32)
    port_node = with_ends(jax.random.randint(splits[5], (N_FZ, PORTS), 0, NODES), jax.random.fold_in(splits[5], 1), 0, NODES - 1).astype(jnp.int32)
    port_conductance = jnp.clip(jnp.exp(math.log(2.0) - 1.3862944 * jax.random.uniform(splits[6], (N_FZ, PORTS), jnp.float32) ** steps_of(splits[6], (N_FZ, PORTS), ((0, 8), (1, 4)), -0.2, 0.2)), 0.5, 2.0)
    inverse = draw_inverse(jax.random.fold_in(splits[14], 71), 0)
    line_near = with_ends(jax.random.randint(splits[8], (N_FZ, LINES), 0, NODES), jax.random.fold_in(splits[8], 1), 0, NODES - 1).astype(jnp.int32)
    line_far = with_ends(jax.random.randint(splits[9], (N_FZ, LINES), 0, NODES), jax.random.fold_in(splits[9], 1), 0, NODES - 1).astype(jnp.int32)
    line_delay = with_ends(jax.random.randint(splits[10], (N_FZ, LINES), 1, DMAX + 1), jax.random.fold_in(splits[10], 1), 1, DMAX).astype(jnp.int32)
    line_imped = jnp.clip(jnp.exp(math.log(4.0) - 2.0794415 * jax.random.uniform(splits[11], (N_FZ, LINES), jnp.float32) ** steps_of(splits[11], (N_FZ, LINES), ((0, 8),), -0.2, 0.2)), 0.5, 4.0)
    hist_near = scatter_about(splits[12], (N_FZ, DMAX, LINES), 1.0, 6.0, ((0, 8),), jnp.float32)
    hist_far = scatter_about(splits[13], (N_FZ, DMAX, LINES), 1.0, 6.0, ((0, 8),), jnp.float32)
    return {"e_field": e_field, "h_field": h_field, "e_decay": e_decay, "e_gain": e_gain, "port_cell": port_cell, "port_node": port_node, "port_conductance": port_conductance, "inverse": inverse, "line_near": line_near, "line_far": line_far, "line_delay": line_delay, "line_imped": line_imped, "hist_near": hist_near, "hist_far": hist_far}


def forward_z(values, upper_face):
    return jnp.concatenate([values[1:], upper_face[None]], 0) - values


def forward_x(values, side_face):
    return jnp.concatenate([values[:, 1:], side_face[:, None]], 1) - values


def forward_y(values):
    return jnp.concatenate([values[:, :, 1:], jnp.zeros_like(values[:, :, :1])], 2) - values


def backward_z(values, lower_face):
    return values - jnp.concatenate([lower_face[None], values[:-1]], 0)


def backward_x(values, side_face):
    return values - jnp.concatenate([side_face[:, None], values[:, :-1]], 1)


def backward_y(values):
    return values - jnp.concatenate([jnp.zeros_like(values[:, :, :1]), values[:, :, :-1]], 2)


def curl_electric(e_field, upper_face, side_face):
    return jnp.stack([
        forward_y(e_field[2]) - forward_z(e_field[1], upper_face[1]),
        forward_z(e_field[0], upper_face[0]) - forward_x(e_field[2], side_face[1]),
        forward_x(e_field[1], side_face[0]) - forward_y(e_field[0])])


def curl_magnetic(h_field, lower_face, side_face):
    return jnp.stack([
        backward_y(h_field[2]) - backward_z(h_field[1], lower_face[1]),
        backward_z(h_field[0], lower_face[0]) - backward_x(h_field[2], side_face[1]),
        backward_x(h_field[1], side_face[0]) - backward_y(h_field[0])])


def reference(e_field, h_field, e_decay, e_gain, port_cell, port_node, port_conductance, inverse,
              line_near, line_far, line_delay, line_imped, hist_near, hist_far):
    row_index = jnp.arange(N_FZ, dtype=jnp.int32)[:, None]
    block_index = jnp.arange(PORTS, dtype=jnp.int32)[None, :] // PORTS_DEV
    z_position = row_index * CZ + port_cell // (CX * NY)
    x_position = block_index * CX + (port_cell // NY) % CX
    y_position = port_cell % NY
    flat_index = ((z_position * NX + x_position) * NY + y_position).astype(jnp.int32)
    gain_flat = e_gain.reshape(-1)
    wave_near = hist_near[:, ::-1]
    wave_far = hist_far[:, ::-1]
    upper_zero = jnp.zeros((2, NX, NY), jnp.float32)
    side_zero = jnp.zeros((2, NZ, NY), jnp.float32)
    empty_nodes = jnp.zeros((N_FZ, NODES), jnp.float32)
    for step_index in range(STEPS):
        position = (step_index - line_delay + DMAX).astype(jnp.int32)[:, None, :]
        incoming_a = jnp.take_along_axis(wave_far, position, axis=1)[:, 0]
        incoming_b = jnp.take_along_axis(wave_near, position, axis=1)[:, 0]
        far_sources = empty_nodes.at[row_index, line_far].add(-incoming_b)
        received = jnp.concatenate([jnp.zeros((1, NODES), jnp.float32), far_sources[:-1]], 0)
        ez_ports = e_field[2].reshape(-1)[flat_index]
        sources = empty_nodes.at[row_index, port_node].add(port_conductance * ez_ports)
        sources = sources + empty_nodes.at[row_index, line_near].add(-incoming_a) + received
        volts = jnp.einsum("snm,sm->sn", inverse, sources, precision=lax.Precision.HIGHEST)
        current = port_conductance * (ez_ports - volts[row_index, port_node])
        e_field = e_decay * e_field + e_gain * curl_magnetic(h_field, upper_zero, side_zero)
        vertical = e_field[2].reshape(-1).at[flat_index].add(-gain_flat[flat_index] * current)
        e_field = e_field.at[2].set(vertical.reshape(e_field.shape[1:]))
        out_near = -2.0 * volts[row_index, line_near] / line_imped - incoming_a
        volts_above = jnp.concatenate([volts[1:], jnp.zeros((1, NODES), jnp.float32)], 0)
        out_far = -2.0 * volts_above[row_index, line_far] / line_imped - incoming_b
        h_field = h_field - 0.5 * curl_electric(e_field, upper_zero, side_zero)
        wave_near = jnp.concatenate([wave_near, out_near[:, None]], 1)
        wave_far = jnp.concatenate([wave_far, out_far[:, None]], 1)
    line_wave = jnp.stack([out_near, out_far], 1)
    return e_field, h_field, volts, line_wave
```

```python
import functools

import jax
import jax.numpy as jnp
from jax import lax
from jax.experimental import pallas as pl
from jax.experimental.pallas import tpu as pltpu
from jax.sharding import PartitionSpec as P

STEPS = 4
LANES = 128
F32 = jnp.float32
BF16 = jnp.bfloat16
MESH = pl.DeviceIdType.MESH


def split3(x):
    a = x.astype(BF16)
    r = x - a.astype(F32)
    b = r.astype(BF16)
    c = (r - b.astype(F32)).astype(BF16)
    return a, b, c


def dot3(x, onehot, transposed):
    rows = x.shape[0]
    dims = (((1,), (1 if transposed else 0,)), ((), ()))
    if rows % 16 == 0:
        y = lax.dot_general(
            jnp.concatenate(split3(x), 0), onehot, dims, preferred_element_type=F32
        )
        return y[:rows] + y[rows : 2 * rows] + y[2 * rows :]
    a, b, c = (
        lax.dot_general(t, onehot, dims, preferred_element_type=F32) for t in split3(x)
    )
    return a + b + c


def kernel(
    e_in, h_in, decay_in, gain_in, port_cell, port_node, port_cond, inv_in,
    line_near, line_far, line_delay, line_imped, hist_near, hist_far,
    e_out, h_out, volt_out, wave_out,
    e, h, decay, gain, inv, cell_row, cell_y, node_hi, node_lo, pads,
    hx_send, hx, ex_send, ex, part_send, part, far_send, far, volt_send, volt,
    up_send, above, acc,
    load_sem, out_sem, face_send, face_recv, part_ss, part_rs, volt_ss, volt_rs,
):
    s, j = lax.axis_index("fz"), lax.axis_index("fxy")
    ns, nj = lax.axis_size("fz"), lax.axis_size("fxy")
    above_id, below_id = lax.rem(s + 1, ns), lax.rem(s + ns - 1, ns)
    right_id, left_id = lax.rem(j + 1, nj), lax.rem(j + nj - 1, nj)
    _, cz, cx, ny = e_in.shape
    cells = cz * cx
    block, nodes = inv_in.shape[1:]
    ports = port_cell.shape[1]
    lines = line_near.shape[1]
    depth = hist_near.shape[1]

    loads = [
        pltpu.make_async_copy(e_in, e.at[:, 0:cz], load_sem.at[0]),
        pltpu.make_async_copy(h_in, h.at[:, 1 : cz + 1], load_sem.at[1]),
        pltpu.make_async_copy(gain_in, gain, load_sem.at[2]),
        pltpu.make_async_copy(inv_in.at[0], inv, load_sem.at[3]),
        pltpu.make_async_copy(decay_in, decay, load_sem.at[4]),
    ]
    for copy in loads:
        copy.start()

    h[:, 0] = jnp.zeros((3, cx, ny), F32)
    e[:, cz] = jnp.zeros((3, cx, ny), F32)
    hx[...] = jnp.zeros(hx.shape, F32)
    ex[...] = jnp.zeros(ex.shape, F32)
    far[...] = jnp.zeros(far.shape, F32)
    above[...] = jnp.zeros(above.shape, F32)

    barrier = pltpu.get_barrier_semaphore()
    for other in (above_id, below_id):
        pl.semaphore_signal(barrier, inc=1, device_id={"fz": other}, device_id_type=MESH)
    for d in range(1, nj):
        pl.semaphore_signal(
            barrier, inc=1, device_id={"fxy": lax.rem(j + d, nj)}, device_id_type=MESH
        )

    pads[...] = jnp.full(pads.shape, -1, jnp.int32)
    pads[0:1, 0:ports] = port_cell[...]
    pads[1:2, 0:ports] = port_node[...]
    cell = pads[0:1, :]
    pnode = pads[1:2, :]
    valid = cell >= 0
    row = jnp.where(valid, cell // ny, -1)
    col = jnp.where(valid, cell % ny, -1)
    cell_row[...] = (lax.broadcasted_iota(jnp.int32, (cells, LANES), 0) == row).astype(F32)
    cell_y[...] = (
        (lax.broadcasted_iota(jnp.int32, (ny, LANES), 0) == col).astype(F32).astype(BF16)
    )
    for k, index in enumerate((pnode, line_near[...], line_far[...])):
        hi = jnp.where(index >= 0, index // block, -1)
        lo = jnp.where(index >= 0, index % block, -1)
        at = pl.ds(k * LANES, LANES)
        node_hi[:, at] = (
            lax.broadcasted_iota(jnp.int32, (node_hi.shape[0], LANES), 0) == hi
        ).astype(F32)
        node_lo[:, at] = (
            (lax.broadcasted_iota(jnp.int32, (block, LANES), 0) == lo)
            .astype(F32)
            .astype(BF16)
        )
    part_send[...] = jnp.zeros(part_send.shape, F32)
    part_send[0, 0:1, 0:ports] = port_cond[...]
    cond = part_send[0, 0:1, 0:LANES]

    has_above, has_below = s < ns - 1, s > 0
    has_right, has_left = j < nj - 1, j > 0

    def face(kind, step, src, dst, axis, other):
        return pltpu.make_async_remote_copy(
            src_ref=src, dst_ref=dst,
            send_sem=face_send.at[kind, step], recv_sem=face_recv.at[kind, step],
            device_id={axis: other}, device_id_type=MESH,
        )

    def up_copies(n):
        return (
            face(0, n, h.at[0:2, cz], h.at[0:2, 0], "fz", above_id),
            face(1, n, hx_send.at[n], hx.at[n], "fxy", right_id),
        )

    def down_copies(n):
        return (
            face(2, n, e.at[0:2, 0], e.at[0:2, cz], "fz", below_id),
            face(3, n, ex_send.at[n], ex.at[n], "fxy", left_id),
        )

    def far_copy(n):
        return face(4, n, far_send.at[n], far.at[n], "fz", above_id)

    def above_copy(n):
        return face(5, n, up_send.at[n], above.at[n], "fz", below_id)

    def start(cond_, copy):
        @pl.when(cond_)
        def _():
            copy.start()

    def wait_recv(cond_, copy):
        @pl.when(cond_)
        def _():
            copy.wait_recv()

    def wait_send(cond_, copy):
        @pl.when(cond_)
        def _():
            copy.wait_send()

    def gather_cells(plane):
        y = dot3(plane.reshape(cells, ny), cell_y[...], False)
        return jnp.sum(y * cell_row[...], axis=0, keepdims=True)

    def gather_nodes(volts, at):
        y = dot3(volts, node_lo[:, at], False)
        return jnp.sum(y * node_hi[0:nj, at], axis=0, keepdims=True)

    def scatter_nodes(values, at):
        rows = node_hi[:, at] * values
        return dot3(rows, node_lo[:, at], True)[0:nj]

    def gathers(n, send, recv, ss, rs):
        return [
            pltpu.make_async_remote_copy(
                src_ref=send.at[n], dst_ref=recv.at[n, j],
                send_sem=ss.at[n, d - 1], recv_sem=rs.at[n, d - 1],
                device_id={"fxy": lax.rem(j + d, nj)}, device_id_type=MESH,
            )
            for d in range(1, nj)
        ]

    at_port = pl.ds(0, LANES)
    at_near = pl.ds(LANES, LANES)
    at_far = pl.ds(2 * LANES, LANES)
    delay = line_delay[...]
    waves_a, waves_b = [], []

    def incoming(n, waves, hist):
        total = jnp.zeros((1, lines), F32)
        for k in range(1, depth + 1):
            value = waves[n - k] if n >= k else hist[0, k - n - 1 : k - n, :]
            total = jnp.where(delay == k, value, total)
        return total

    def send_far(n, in_b):
        far_send[n] = scatter_nodes(-in_b, at_far)
        start(has_above, far_copy(n))

    def send_ports(n):
        ez = gather_cells(e[2, 0:cz])
        own = scatter_nodes(cond * ez, at_port)
        part_send[n] = own
        for copy in gathers(n, part_send, part, part_ss, part_rs):
            copy.start()
        return ez, own

    lane = lax.broadcasted_iota(jnp.int32, (cx, ny), 1)
    sub = lax.broadcasted_iota(jnp.int32, (cx, ny), 0)

    in_b = incoming(0, waves_a, hist_near)
    in_a = incoming(0, waves_b, hist_far)
    pl.semaphore_wait(barrier, nj + 1)
    send_far(0, in_b)
    loads[0].wait()
    ez, own = send_ports(0)
    loads[1].wait()
    for c in range(2):
        for z in range(cz):
            hx_send[0, c, z : z + 1, :] = h[1 + c, z + 1, cx - 1 : cx, :]
    copy_z, copy_x = up_copies(0)
    start(has_above, copy_z)
    start(has_right, copy_x)
    loads[2].wait()
    gain_port = gather_cells(gain[...])
    loads[3].wait()
    loads[4].wait()

    for n in range(STEPS):
        near_src = scatter_nodes(-in_a, at_near)
        wait_recv(has_below, far_copy(n))
        port_copies = gathers(n, part_send, part, part_ss, part_rs)
        for copy in port_copies:
            copy.wait_recv()
        part[n, j] = own
        totals = part[n, 0]
        for k in range(1, nj):
            totals = totals + part[n, k]
        totals = totals + (near_src + far[n])
        chunk = 32

        @pl.loop(0, block // chunk)
        def _(r):
            at = pl.ds(pl.multiple_of(r * chunk, chunk), chunk)
            value = jnp.zeros((chunk, LANES), F32)
            for k in range(nodes // LANES):
                q, w = divmod(k * LANES, block)
                value = value + inv[at, k * LANES : (k + 1) * LANES] * totals[
                    q : q + 1, w : w + LANES
                ]
            acc[at, :] = value

        terms = jnp.concatenate(split3(acc[...]), 1)
        local_volt = lax.dot_general(
            jnp.ones((16, 3 * LANES), BF16), terms, (((1,), (1,)), ((), ())),
            preferred_element_type=F32,
        )[0:1]
        volt_send[n] = local_volt
        volt_copies = gathers(n, volt_send, volt, volt_ss, volt_rs)
        for copy in volt_copies:
            copy.start()

        copy_z, copy_x = up_copies(n)
        wait_recv(has_below, copy_z)
        wait_recv(has_left, copy_x)

        @pl.loop(0, cz)
        def _(z):
            hx_, hy_, hz_ = (h[c, z + 1] for c in range(3))
            lx, ly = h[0, z], h[1, z]
            fy = hx[n, 0, pl.ds(z, 1), :]
            fz = hx[n, 1, pl.ds(z, 1), :]

            def by(f):
                return f - jnp.where(lane == 0, 0.0, pltpu.roll(f, 1, 1))

            def bx(f, side):
                return f - jnp.where(sub == 0, side, pltpu.roll(f, 1, 0))

            g, q = gain[z], decay[z]
            e[0, z] = q * e[0, z] + g * (by(hz_) - (hy_ - ly))
            e[1, z] = q * e[1, z] + g * ((hx_ - lx) - bx(hz_, fz))
            e[2, z] = q * e[2, z] + g * (bx(hy_, fy) - by(hx_))

        for copy in volt_copies:
            copy.wait_recv()
        volt[n, j] = local_volt
        volts = jnp.concatenate([volt[n, k] for k in range(nj)], 0)
        up_send[n] = volts
        start(has_below, above_copy(n))
        drop = gain_port * (cond * (ez - gather_nodes(volts, at_port)))
        change = dot3(cell_row[...] * drop, cell_y[...], True)
        e[2, 0:cz] = e[2, 0:cz] - change.reshape(cz, cx, ny)
        for c in range(2):
            for z in range(cz):
                ex_send[n, c, z : z + 1, :] = e[1 + c, z, 0:1, :]
        down_z, down_x = down_copies(n)
        start(has_below, down_z)
        start(has_left, down_x)

        out_a = -2.0 * gather_nodes(volts, at_near) / line_imped[...] - in_a
        waves_a.append(out_a)
        old_b, old_ez = in_b, ez
        if n + 1 < STEPS:
            ez, own = send_ports(n + 1)
            in_b = incoming(n + 1, waves_a, hist_near)
            send_far(n + 1, in_b)
        else:
            e_store = pltpu.make_async_copy(e.at[:, 0:cz], e_out, out_sem.at[0])
            e_store.start()

        wait_send(has_above, copy_z)
        wait_send(has_right, copy_x)
        wait_recv(has_above, down_z)
        wait_recv(has_right, down_x)

        @pl.loop(0, cz)
        def _(z):
            ex_, ey_, ez_ = (e[c, z] for c in range(3))
            ux, uy = e[0, z + 1], e[1, z + 1]
            fy = ex[n, 0, pl.ds(z, 1), :]
            fz = ex[n, 1, pl.ds(z, 1), :]

            def dy(f):
                return jnp.where(lane == ny - 1, 0.0, pltpu.roll(f, ny - 1, 1)) - f

            def dx(f, side):
                return jnp.where(sub == cx - 1, side, pltpu.roll(f, cx - 1, 0)) - f

            h[0, z + 1] = h[0, z + 1] - 0.5 * (dy(ez_) - (uy - ey_))
            new_y = h[1, z + 1] - 0.5 * ((ux - ex_) - dx(ez_, fz))
            new_z = h[2, z + 1] - 0.5 * (dx(ey_, fy) - dy(ex_))
            h[1, z + 1] = new_y
            h[2, z + 1] = new_z
            if n + 1 < STEPS:
                hx_send[n + 1, 0, pl.ds(z, 1), :] = new_y[cx - 1 : cx, :]
                hx_send[n + 1, 1, pl.ds(z, 1), :] = new_z[cx - 1 : cx, :]

        if n + 1 < STEPS:
            next_z, next_x = up_copies(n + 1)
            start(has_above, next_z)
            start(has_right, next_x)
        else:
            h_store = pltpu.make_async_copy(h.at[:, 1 : cz + 1], h_out, out_sem.at[1])
            h_store.start()

        wait_recv(has_above, above_copy(n))
        out_b = -2.0 * gather_nodes(above[n], at_far) / line_imped[...] - old_b
        waves_b.append(out_b)
        if n + 1 < STEPS:
            in_a = incoming(n + 1, waves_b, hist_far)

        wait_send(has_below, down_z)
        wait_send(has_left, down_x)
        wait_send(has_above, far_copy(n))
        wait_send(has_below, above_copy(n))
        for copy in port_copies + volt_copies:
            copy.wait_send()

    volt_out[...] = local_volt
    wave_out[0, 0:1, :] = out_a
    wave_out[0, 1:2, :] = out_b
    e_store.wait()
    h_store.wait()


def local(*args):
    e_field, inverse = args[0], args[7]
    nj = lax.axis_size("fxy")
    _, cz, cx, ny = e_field.shape
    _, block, nodes = inverse.shape
    lines = args[8].shape[1]
    vmem, any_ = pl.BlockSpec(memory_space=pltpu.VMEM), pl.BlockSpec(memory_space=pl.ANY)
    in_any = (0, 1, 2, 3, 7)
    rows = -(-nj // 16) * 16
    dma = pltpu.SemaphoreType.DMA
    v = pltpu.VMEM
    return pl.pallas_call(
        kernel,
        out_shape=(
            jax.ShapeDtypeStruct(e_field.shape, F32),
            jax.ShapeDtypeStruct(e_field.shape, F32),
            jax.ShapeDtypeStruct((1, block), F32),
            jax.ShapeDtypeStruct((1, 2, lines), F32),
        ),
        in_specs=[any_ if i in in_any else vmem for i in range(len(args))],
        out_specs=(any_, any_, vmem, vmem),
        scratch_shapes=[
            v((3, cz + 1, cx, ny), F32),
            v((3, cz + 1, cx, ny), F32),
            v((cz, cx, ny), F32),
            v((cz, cx, ny), F32),
            v((block, nodes), F32),
            v((cz * cx, LANES), F32),
            v((ny, LANES), BF16),
            v((rows, 3 * LANES), F32),
            v((block, 3 * LANES), BF16),
            v((8, LANES), jnp.int32),
            v((STEPS, 2, cz, ny), F32),
            v((STEPS, 2, cz, ny), F32),
            v((STEPS, 2, cz, ny), F32),
            v((STEPS, 2, cz, ny), F32),
            v((STEPS, nj, block), F32),
            v((STEPS, nj, nj, block), F32),
            v((STEPS, nj, block), F32),
            v((STEPS, nj, block), F32),
            v((STEPS, 1, block), F32),
            v((STEPS, nj, 1, block), F32),
            v((STEPS, nj, block), F32),
            v((STEPS, nj, block), F32),
            v((block, LANES), F32),
            dma((5,)),
            dma((2,)),
            dma((6, STEPS)),
            dma((6, STEPS)),
            dma((STEPS, nj - 1)),
            dma((STEPS, nj - 1)),
            dma((STEPS, nj - 1)),
            dma((STEPS, nj - 1)),
        ],
        compiler_params=pltpu.CompilerParams(
            collective_id=0, has_side_effects=True, vmem_limit_bytes=48 * 1024 * 1024
        ),
    )(*args)


def solution(mesh):
    placed = (
        P(None, "fz", "fxy", None),
        P(None, "fz", "fxy", None),
        P("fz", "fxy", None),
        P("fz", "fxy", None),
        P("fz", "fxy"),
        P("fz", "fxy"),
        P("fz", "fxy"),
        P("fz", "fxy", None),
        P("fz", None),
        P("fz", None),
        P("fz", None),
        P("fz", None),
        P("fz", None, None),
        P("fz", None, None),
    )
    return jax.shard_map(
        local,
        mesh=mesh,
        in_specs=placed,
        out_specs=(
            P(None, "fz", "fxy", None),
            P(None, "fz", "fxy", None),
            P("fz", "fxy"),
            P("fz", None, None),
        ),
        check_vma=False,
    )
```

```python
import functools

import jax
import jax.numpy as jnp
from jax import lax
from jax.experimental import pallas as pl
from jax.experimental.pallas import tpu as pltpu
from jax.sharding import PartitionSpec as P

STEPS = 4
LANES = 128
F32 = jnp.float32
BF16 = jnp.bfloat16
MESH = pl.DeviceIdType.MESH


def split3(x):
    a = x.astype(BF16)
    r = x - a.astype(F32)
    b = r.astype(BF16)
    c = (r - b.astype(F32)).astype(BF16)
    return a, b, c


def dot3(x, onehot, transposed):
    rows = x.shape[0]
    dims = (((1,), (1 if transposed else 0,)), ((), ()))
    if rows % 16 == 0:
        y = lax.dot_general(
            jnp.concatenate(split3(x), 0), onehot, dims, preferred_element_type=F32
        )
        return y[:rows] + y[rows : 2 * rows] + y[2 * rows :]
    a, b, c = (
        lax.dot_general(t, onehot, dims, preferred_element_type=F32) for t in split3(x)
    )
    return a + b + c


def kernel(
    e_in, h_in, decay_in, gain_in, port_cell_in, port_node_in, port_cond_in, inv_in,
    line_near_in, line_far_in, line_delay_in, line_imped_in, hist_near_in, hist_far_in,
    e_out, h_out, volt_out, wave_out,
    port_cell, port_node, port_cond, line_near, line_far, line_delay, line_imped,
    hist_near, hist_far,
    e, h, hz, ez_up, decay, gain, inv, cell_row, cell_y, node_hi, node_lo, pads,
    hx_send, hx, ex_send, ex, part_send, part, far_send, far, volt_send, volt,
    up_send, above, acc,
    load_sem, out_sem, face_send, face_recv, part_ss, part_rs, volt_ss, volt_rs,
):
    s, j = lax.axis_index("fz"), lax.axis_index("fxy")
    ns, nj = lax.axis_size("fz"), lax.axis_size("fxy")
    above_id, below_id = lax.rem(s + 1, ns), lax.rem(s + ns - 1, ns)
    right_id, left_id = lax.rem(j + 1, nj), lax.rem(j + nj - 1, nj)
    _, cz, cx, ny = e_in.shape
    cells = cz * cx
    block, nodes = inv_in.shape[1:]
    ports = port_cell_in.shape[1]
    lines = line_near_in.shape[1]
    depth = hist_near_in.shape[0]

    loads = [
        pltpu.make_async_copy(e_in, e.at[:, 0:cz], load_sem.at[0]),
        pltpu.make_async_copy(h_in, h.at[:, 1 : cz + 1], load_sem.at[1]),
        pltpu.make_async_copy(gain_in, gain, load_sem.at[2]),
        pltpu.make_async_copy(inv_in.at[0], inv, load_sem.at[3]),
        pltpu.make_async_copy(decay_in, decay, load_sem.at[4]),
    ]
    small = (
        (port_cell_in, port_cell), (port_node_in, port_node), (port_cond_in, port_cond),
        (line_near_in, line_near), (line_far_in, line_far), (line_delay_in, line_delay),
        (line_imped_in, line_imped), (hist_near_in, hist_near), (hist_far_in, hist_far),
    )
    small = [
        pltpu.make_async_copy(src, dst, load_sem.at[5 + k])
        for k, (src, dst) in enumerate(small)
    ]
    for copy in small + loads:
        copy.start()

    h[:, 0] = jnp.zeros((3, cx, ny), F32)
    e[:, cz] = jnp.zeros((3, cx, ny), F32)
    far[...] = jnp.zeros(far.shape, F32)
    above[...] = jnp.zeros(above.shape, F32)

    barrier = pltpu.get_barrier_semaphore()
    for other in (above_id, below_id):
        pl.semaphore_signal(barrier, inc=1, device_id={"fz": other}, device_id_type=MESH)
    for d in range(1, nj):
        pl.semaphore_signal(
            barrier, inc=1, device_id={"fxy": lax.rem(j + d, nj)}, device_id_type=MESH
        )

    for copy in small:
        copy.wait()

    pads[...] = jnp.full(pads.shape, -1, jnp.int32)
    pads[0:1, 0:ports] = port_cell[...]
    pads[1:2, 0:ports] = port_node[...]
    cell = pads[0:1, :]
    pnode = pads[1:2, :]
    valid = cell >= 0
    row = jnp.where(valid, cell // ny, -1)
    col = jnp.where(valid, cell % ny, -1)
    cell_row[...] = (lax.broadcasted_iota(jnp.int32, (cells, LANES), 0) == row).astype(F32)
    cell_y[...] = (
        (lax.broadcasted_iota(jnp.int32, (ny, LANES), 0) == col).astype(F32).astype(BF16)
    )
    for k, index in enumerate((pnode, line_near[...], line_far[...])):
        hi = jnp.where(index >= 0, index // block, -1)
        lo = jnp.where(index >= 0, index % block, -1)
        at = pl.ds(k * LANES, LANES)
        node_hi[:, at] = (
            lax.broadcasted_iota(jnp.int32, (node_hi.shape[0], LANES), 0) == hi
        ).astype(F32)
        node_lo[:, at] = (
            (lax.broadcasted_iota(jnp.int32, (block, LANES), 0) == lo)
            .astype(F32)
            .astype(BF16)
        )
    part_send[...] = jnp.zeros(part_send.shape, F32)
    part_send[0, 0:1, 0:ports] = port_cond[...]
    cond = part_send[0, 0:1, 0:LANES]

    has_above, has_below = s < ns - 1, s > 0
    has_right, has_left = j < nj - 1, j > 0

    def face(kind, step, src, dst, axis, other):
        return pltpu.make_async_remote_copy(
            src_ref=src, dst_ref=dst,
            send_sem=face_send.at[kind, step], recv_sem=face_recv.at[kind, step],
            device_id={axis: other}, device_id_type=MESH,
        )

    def up_copies(n):
        return (
            face(0, n, h.at[0:2, cz], hz.at[n], "fz", above_id),
            face(1, n, hx_send.at[n], hx.at[n], "fxy", right_id),
        )

    def down_copies(n):
        return (
            face(2, n, e.at[0:2, 0], ez_up.at[n], "fz", below_id),
            face(3, n, ex_send.at[n], ex.at[n], "fxy", left_id),
        )

    def far_copy(n):
        return face(4, n, far_send.at[n], far.at[n], "fz", above_id)

    def above_copy(n):
        return face(5, n, up_send.at[n], above.at[n], "fz", below_id)

    def start(cond_, copy):
        @pl.when(cond_)
        def _():
            copy.start()

    def wait_recv(cond_, copy):
        @pl.when(cond_)
        def _():
            copy.wait_recv()

    def wait_send(cond_, copy):
        @pl.when(cond_)
        def _():
            copy.wait_send()

    def gather_cells(plane):
        y = dot3(plane.reshape(cells, ny), cell_y[...], False)
        return jnp.sum(y * cell_row[...], axis=0, keepdims=True)

    def gather_nodes(volts, at):
        y = dot3(volts, node_lo[:, at], False)
        return jnp.sum(y * node_hi[0:nj, at], axis=0, keepdims=True)

    def scatter_nodes(values, at):
        rows = node_hi[:, at] * values
        return dot3(rows, node_lo[:, at], True)[0:nj]

    def gathers(n, send, recv, ss, rs):
        return [
            pltpu.make_async_remote_copy(
                src_ref=send.at[n], dst_ref=recv.at[n, j],
                send_sem=ss.at[n, d - 1], recv_sem=rs.at[n, d - 1],
                device_id={"fxy": lax.rem(j + d, nj)}, device_id_type=MESH,
            )
            for d in range(1, nj)
        ]

    at_port = pl.ds(0, LANES)
    at_near = pl.ds(LANES, LANES)
    at_far = pl.ds(2 * LANES, LANES)
    delay = line_delay[...]
    waves_a, waves_b = [], []

    def incoming(n, waves, hist):
        total = jnp.zeros((1, lines), F32)
        for k in range(1, depth + 1):
            value = waves[n - k] if n >= k else hist[k - n - 1]
            total = jnp.where(delay == k, value, total)
        return total

    def send_far(n, in_b):
        far_send[n] = scatter_nodes(-in_b, at_far)
        start(has_above, far_copy(n))

    def send_ports(n):
        ez = gather_cells(e[2, 0:cz])
        own = scatter_nodes(cond * ez, at_port)
        part_send[n] = own
        for copy in gathers(n, part_send, part, part_ss, part_rs):
            copy.start()
        return ez, own

    lane = lax.broadcasted_iota(jnp.int32, (cx, ny), 1)
    sub = lax.broadcasted_iota(jnp.int32, (cx, ny), 0)

    in_b = incoming(0, waves_a, hist_near)
    in_a = incoming(0, waves_b, hist_far)
    pl.semaphore_wait(barrier, nj + 1)
    send_far(0, in_b)
    loads[0].wait()
    ez, own = send_ports(0)
    loads[1].wait()
    for c in range(2):
        for z in range(cz):
            hx_send[0, c, z : z + 1, :] = h[1 + c, z + 1, cx - 1 : cx, :]
    copy_z, copy_x = up_copies(0)
    start(has_above, copy_z)
    start(has_right, copy_x)
    loads[2].wait()
    gain_port = gather_cells(gain[...])
    loads[3].wait()
    loads[4].wait()

    for n in range(STEPS):
        near_src = scatter_nodes(-in_a, at_near)
        wait_recv(has_below, far_copy(n))
        port_copies = gathers(n, part_send, part, part_ss, part_rs)
        for copy in port_copies:
            copy.wait_recv()
        part[n, j] = own
        totals = part[n, 0]
        for k in range(1, nj):
            totals = totals + part[n, k]
        totals = totals + (near_src + far[n])
        chunk = 32

        @pl.loop(0, block // chunk)
        def _(r):
            at = pl.ds(pl.multiple_of(r * chunk, chunk), chunk)
            value = jnp.zeros((chunk, LANES), F32)
            for k in range(nodes // LANES):
                q, w = divmod(k * LANES, block)
                value = value + inv[at, k * LANES : (k + 1) * LANES] * totals[
                    q : q + 1, w : w + LANES
                ]
            acc[at, :] = value

        terms = jnp.concatenate(split3(acc[...]), 1)
        local_volt = lax.dot_general(
            jnp.ones((16, 3 * LANES), BF16), terms, (((1,), (1,)), ((), ())),
            preferred_element_type=F32,
        )[0:1]
        volt_send[n] = local_volt
        volt_copies = gathers(n, volt_send, volt, volt_ss, volt_rs)
        for copy in volt_copies:
            copy.start()

        copy_z, copy_x = up_copies(n)

        @pl.loop(0, cz)
        def _(z):
            hx_, hy_, hz_ = (h[c, z + 1] for c in range(3))
            lx, ly = h[0, z], h[1, z]

            def by(f):
                return f - jnp.where(lane == 0, 0.0, pltpu.roll(f, 1, 1))

            def bx(f):
                return f - jnp.where(sub == 0, 0.0, pltpu.roll(f, 1, 0))

            g, q = gain[z], decay[z]
            e[0, z] = q * e[0, z] + g * (by(hz_) - (hy_ - ly))
            e[1, z] = q * e[1, z] + g * ((hx_ - lx) - bx(hz_))
            e[2, z] = q * e[2, z] + g * (bx(hy_) - by(hx_))

        down_z, down_x = down_copies(n)

        @pl.when(has_left)
        def _():
            copy_x.wait_recv()
            for z in range(cz):
                g = gain[z, 0:1, :]
                e[1, z, 0:1, :] = e[1, z, 0:1, :] + g * hx[n, 1, z : z + 1, :]
                e[2, z, 0:1, :] = e[2, z, 0:1, :] - g * hx[n, 0, z : z + 1, :]

        @pl.when(has_below)
        def _():
            copy_z.wait_recv()
            g = gain[0]
            e[0, 0] = e[0, 0] + g * hz[n, 1]
            e[1, 0] = e[1, 0] - g * hz[n, 0]
            down_z.start()

        for copy in volt_copies:
            copy.wait_recv()
        volt[n, j] = local_volt
        volts = jnp.concatenate([volt[n, k] for k in range(nj)], 0)
        up_send[n] = volts
        start(has_below, above_copy(n))
        drop = gain_port * (cond * (ez - gather_nodes(volts, at_port)))
        change = dot3(cell_row[...] * drop, cell_y[...], True)
        e[2, 0:cz] = e[2, 0:cz] - change.reshape(cz, cx, ny)
        for c in range(2):
            for z in range(cz):
                ex_send[n, c, z : z + 1, :] = e[1 + c, z, 0:1, :]
        start(has_left, down_x)

        out_a = -2.0 * gather_nodes(volts, at_near) / line_imped[...] - in_a
        waves_a.append(out_a)
        old_b, old_ez = in_b, ez
        if n + 1 < STEPS:
            ez, own = send_ports(n + 1)
            in_b = incoming(n + 1, waves_a, hist_near)
            send_far(n + 1, in_b)
        else:
            e_store = pltpu.make_async_copy(e.at[:, 0:cz], e_out, out_sem.at[0])
            e_store.start()

        wait_send(has_above, copy_z)
        wait_send(has_right, copy_x)

        @pl.loop(0, cz)
        def _(z):
            ex_, ey_, ez_ = (e[c, z] for c in range(3))
            ux, uy = e[0, z + 1], e[1, z + 1]

            def dy(f):
                return jnp.where(lane == ny - 1, 0.0, pltpu.roll(f, ny - 1, 1)) - f

            def dx(f):
                return jnp.where(sub == cx - 1, 0.0, pltpu.roll(f, cx - 1, 0)) - f

            h[0, z + 1] = h[0, z + 1] - 0.5 * (dy(ez_) - (uy - ey_))
            h[1, z + 1] = h[1, z + 1] - 0.5 * ((ux - ex_) - dx(ez_))
            h[2, z + 1] = h[2, z + 1] - 0.5 * (dx(ey_) - dy(ex_))

        @pl.when(has_above)
        def _():
            down_z.wait_recv()
            h[0, cz] = h[0, cz] + 0.5 * ez_up[n, 1]
            h[1, cz] = h[1, cz] - 0.5 * ez_up[n, 0]

        if n + 1 < STEPS:
            next_z, next_x = up_copies(n + 1)
        at_x = slice(cx - 1, cx)

        @pl.when(has_right)
        def _():
            down_x.wait_recv()
            for z in range(cz):
                new_y = h[1, z + 1, at_x, :] + 0.5 * ex[n, 1, z : z + 1, :]
                new_z = h[2, z + 1, at_x, :] - 0.5 * ex[n, 0, z : z + 1, :]
                h[1, z + 1, at_x, :] = new_y
                h[2, z + 1, at_x, :] = new_z
                if n + 1 < STEPS:
                    hx_send[n + 1, 0, z : z + 1, :] = new_y
                    hx_send[n + 1, 1, z : z + 1, :] = new_z
            if n + 1 < STEPS:
                next_x.start()

        if n + 1 < STEPS:
            start(has_above, next_z)
        else:
            h_store = pltpu.make_async_copy(h.at[:, 1 : cz + 1], h_out, out_sem.at[1])
            h_store.start()

        wait_recv(has_above, above_copy(n))
        out_b = -2.0 * gather_nodes(above[n], at_far) / line_imped[...] - old_b
        waves_b.append(out_b)
        if n + 1 < STEPS:
            in_a = incoming(n + 1, waves_b, hist_far)

        wait_send(has_below, down_z)
        wait_send(has_left, down_x)
        wait_send(has_above, far_copy(n))
        wait_send(has_below, above_copy(n))
        for copy in port_copies + volt_copies:
            copy.wait_send()

    volt_out[...] = local_volt
    wave_out[0, 0:1, :] = out_a
    wave_out[0, 1:2, :] = out_b
    e_store.wait()
    h_store.wait()


def local(*args):
    e_field, inverse = args[0], args[7]
    nj = lax.axis_size("fxy")
    _, cz, cx, ny = e_field.shape
    _, block, nodes = inverse.shape
    lines = args[8].shape[1]
    args = [*args[:12], *(a.transpose(1, 0, 2) for a in args[12:])]
    vmem, any_ = pl.BlockSpec(memory_space=pltpu.VMEM), pl.BlockSpec(memory_space=pl.ANY)
    small = [a for i, a in enumerate(args) if i not in (0, 1, 2, 3, 7)]
    hbm = pl.BlockSpec(memory_space=pltpu.HBM)
    rows = -(-nj // 16) * 16
    dma = pltpu.SemaphoreType.DMA
    v = pltpu.VMEM
    return pl.pallas_call(
        kernel,
        out_shape=(
            jax.ShapeDtypeStruct(e_field.shape, F32),
            jax.ShapeDtypeStruct(e_field.shape, F32),
            jax.ShapeDtypeStruct((1, block), F32),
            jax.ShapeDtypeStruct((1, 2, lines), F32),
        ),
        in_specs=[hbm] * len(args),
        out_specs=(any_, any_, vmem, vmem),
        scratch_shapes=[
            *[v(a.shape, a.dtype) for a in small],
            v((3, cz + 1, cx, ny), F32),
            v((3, cz + 1, cx, ny), F32),
            v((STEPS, 2, cx, ny), F32),
            v((STEPS, 2, cx, ny), F32),
            v((cz, cx, ny), F32),
            v((cz, cx, ny), F32),
            v((block, nodes), F32),
            v((cz * cx, LANES), F32),
            v((ny, LANES), BF16),
            v((rows, 3 * LANES), F32),
            v((block, 3 * LANES), BF16),
            v((8, LANES), jnp.int32),
            v((STEPS, 2, cz, ny), F32),
            v((STEPS, 2, cz, ny), F32),
            v((STEPS, 2, cz, ny), F32),
            v((STEPS, 2, cz, ny), F32),
            v((STEPS, nj, block), F32),
            v((STEPS, nj, nj, block), F32),
            v((STEPS, nj, block), F32),
            v((STEPS, nj, block), F32),
            v((STEPS, 1, block), F32),
            v((STEPS, nj, 1, block), F32),
            v((STEPS, nj, block), F32),
            v((STEPS, nj, block), F32),
            v((block, LANES), F32),
            dma((5 + len(small),)),
            dma((2,)),
            dma((6, STEPS)),
            dma((6, STEPS)),
            dma((STEPS, nj - 1)),
            dma((STEPS, nj - 1)),
            dma((STEPS, nj - 1)),
            dma((STEPS, nj - 1)),
        ],
        compiler_params=pltpu.CompilerParams(
            collective_id=0, has_side_effects=True, vmem_limit_bytes=67043328
        ),
    )(*args)


def solution(mesh):
    placed = (
        P(None, "fz", "fxy", None),
        P(None, "fz", "fxy", None),
        P("fz", "fxy", None),
        P("fz", "fxy", None),
        P("fz", "fxy"),
        P("fz", "fxy"),
        P("fz", "fxy"),
        P("fz", "fxy", None),
        P("fz", None),
        P("fz", None),
        P("fz", None),
        P("fz", None),
        P("fz", None, None),
        P("fz", None, None),
    )
    return jax.shard_map(
        local,
        mesh=mesh,
        in_specs=placed,
        out_specs=(
            P(None, "fz", "fxy", None),
            P(None, "fz", "fxy", None),
            P("fz", "fxy"),
            P("fz", None, None),
        ),
        check_vma=False,
    )
```
